32 devices in a mesh: groups: 2 (over x), seq: 8 (over z, y), tensor: 2 (over core).
Axes of the slice: x: 2, y: 2, z: 4, core: 2. Of those that a mesh axis runs over, the one named last changes fastest.
Arguments:
- queries: bfloat16 [128, 2, 8192], P(('groups', 'seq'), None, 'tensor'), parts along dimension 0, may hold values from -384 to 384
- fresh_keys: bfloat16 [128, 2, 1024], P(('groups', 'seq'), None, 'tensor'), parts along dimension 0, may hold values from -24 to 24
- fresh_values: bfloat16 [128, 2, 1024], P(('groups', 'seq'), None, 'tensor'), parts along dimension 0, may hold values from -6 to 6
- residual_in: bfloat16 [128, 2, 8192], P(('groups', 'seq'), None, 'tensor'), parts along dimension 0, may hold values from -0.29882812 to 0.29882812
- cache_keys: bfloat16 [8, 8192, 128], P('tensor', ('groups', 'seq')), parts along dimension 1, may hold values from -8 to 8
- cache_values: bfloat16 [8, 8192, 128], P('tensor', ('groups', 'seq')), parts along dimension 1, may hold values from -6 to 6
- key_scales: float32 [8, 128], P('tensor', ('groups', 'seq')), parts along dimension 1, may hold values from 0.5 to 2
- value_scales: float32 [8, 128], P('tensor', ('groups', 'seq')), parts along dimension 1, may hold values from 0.5 to 2
- page_table: int32 [16, 8], P(('groups', 'seq')), parts along dimension 0, may hold values from 0 to 7, each once within a row
- row_lengths: int32 [128], P('groups'), parts along dimension 0, may hold values from 512 to 4096
- norm_gain: float32 [8192], P('tensor'), may hold values from 0.1 to 1.9
- w_gate: bfloat16 [8192, 14336], P('tensor', 'seq'), may hold values from -0.0625 to 0.0625
- w_up: bfloat16 [8192, 14336], P('tensor', 'seq'), may hold values from -0.0625 to 0.0625
- w_down: bfloat16 [14336, 8192], P('seq', 'tensor'), may hold values from -0.046875 to 0.046875
Outputs:
- layer_out: bfloat16 [128, 2, 8192], P(('groups', 'seq'), None, 'tensor'), parts along dimension 0
The draws below stay inside these ranges and needn't reach their ends.
There are 2 independent parts, one for each index of `groups`. The reference program is written for one: setup_inputs(seed, part) draws one part's arguments, and reference() takes and returns one part's arrays. A program takes and returns all parts, laid end to end along the dimension named above; an argument that names none is the same for every part. Nothing has to cross between parts.
Inputs may be any that keep to these rules, and one draw needn't show every extreme that they name: Each row of page_table names each of its seq index's pages once. `row_lengths`: every row sees at least the cache positions of the first seq index.
All inputs are finite; a program needn't handle non-finite values.
Results may differ from the reference program's by a relative error of at most 0.0064.
Values may be sent and summed in bfloat16 or wider, within the bound.
No kernel may reach another device: no remote copies, remote signals or barrier semaphores. Data moves between devices by JAX's collectives and lax.ppermute only.
A program may use at most 128 MiB of HBM per device.

```python
import math
import jax
import jax.numpy as jnp
from jax import lax

D = 8192
H = 64
KVH = 8
HD = 128
FF = 14336
ROWS = 64
STEPS = 2
BLK = 64
CACHE_DEV = 512
CACHE = 4096
BPD = 8
N_SEQ = 8


def drawn_pair(key):
    base_key = jax.random.fold_in(key, 11)
    key_draw = jax.random.fold_in(base_key, 1)
    query_draw = jax.random.fold_in(base_key, 2)
    cache_rows = jnp.clip(jax.random.normal(key_draw, (KVH, CACHE, HD), jnp.float32), -6.0, 6.0)
    query_rows = jnp.clip(2.0 * jax.random.normal(query_draw, (ROWS, STEPS, D), jnp.float32), -12.0, 12.0)
    return (cache_rows, query_rows)


def draw_cache_keys(key, part):
    return drawn_pair(key)[0].astype(jnp.bfloat16)


def draw_queries(key, part):
    return drawn_pair(key)[1].astype(jnp.bfloat16)


def place_ends(result, rng, least, high):
    extent = result.shape
    index_at = [jax.random.randint(jax.random.fold_in(rng, axis), (), 0, extent[axis]) for axis in range(len(extent))]
    result = result.at[tuple(index_at)].set(least)
    longest = extent.index(max(extent))
    index_at[longest] = (index_at[longest] + 1) % extent[longest]
    return result.at[tuple(index_at)].set(high)


def levels(key, extent, pieces, least, high):
    def one(axis_at, parts):
        draws = jax.random.uniform(jax.random.fold_in(jax.random.fold_in(key, 6), axis_at), (parts,), jnp.float32, least / len(pieces), high / len(pieces))
        return jnp.repeat(jnp.exp(draws), extent[axis_at] // parts).reshape((-1,) + (1,) * (len(extent) - axis_at - 1))

    loudness = one(*pieces[0])
    for cut in pieces[1:]:
        loudness = loudness * one(*cut)
    return loudness


def bell_draw(stream_key, dims, spread, bound, shards=(), kind=jnp.bfloat16):
    values = spread * jax.random.normal(stream_key, dims, jnp.float32)
    if shards:
        values = values * levels(stream_key, dims, shards, -0.22, 0.18)
    return jnp.clip(values, -bound, bound).astype(kind)


def setup_inputs(seed: int = 0, part: int = 0) -> dict:
    seeds = jax.random.split(jax.random.key(seed), 15)
    own_keys = jax.random.split(jax.random.fold_in(seeds[14], part), 15)
    return {
        "queries": draw_queries(jax.random.fold_in(jax.random.fold_in(seeds[14], part), 71), part),
        "fresh_keys": bell_draw(own_keys[1], (ROWS, STEPS, KVH * HD), 4.0, 24.0, ((0, 8), (2, 2))),
        "fresh_values": bell_draw(own_keys[2], (ROWS, STEPS, KVH * HD), 1.0, 6.0, ((0, 8), (2, 2))),
        "residual_in": bell_draw(own_keys[3], (ROWS, STEPS, D), 0.05, 0.29882812, ((0, 8), (2, 2))),
        "cache_keys": draw_cache_keys(jax.random.fold_in(jax.random.fold_in(seeds[14], part), 71), part),
        "cache_values": bell_draw(own_keys[5], (KVH, CACHE, HD), 1.0, 6.0, ((0, 2), (1, 8))),
        "key_scales": jnp.clip(jnp.exp(math.log(2.0) - 1.3862944 * jax.random.uniform(own_keys[6], (KVH, CACHE // BLK), jnp.float32) ** levels(own_keys[6], (KVH, CACHE // BLK), ((0, 2), (1, 8)), -0.2, 0.2)), 0.5, 2.0),
        "value_scales": jnp.clip(jnp.exp(math.log(2.0) - 1.3862944 * jax.random.uniform(own_keys[7], (KVH, CACHE // BLK), jnp.float32) ** levels(own_keys[7], (KVH, CACHE // BLK), ((0, 2), (1, 8)), -0.2, 0.2)), 0.5, 2.0),
        "page_table": jax.vmap(lambda own: jax.random.permutation(own, BPD))(jax.random.split(own_keys[8], N_SEQ)).reshape((N_SEQ, BPD)).astype(jnp.int32),
        "row_lengths": place_ends(jax.random.randint(own_keys[9], (ROWS,), CACHE_DEV, CACHE + 1), jax.random.fold_in(own_keys[9], 1), CACHE_DEV, CACHE).astype(jnp.int32),
        "norm_gain": jnp.clip(1.0 + 0.18 * jax.random.normal(seeds[10], (D,), jnp.float32), 0.1, 1.9),
        "w_gate": bell_draw(seeds[11], (D, FF), D ** -0.5, 0.0625, ((0, 2), (1, 8))),
        "w_up": bell_draw(seeds[12], (D, FF), D ** -0.5, 0.0625, ((0, 2), (1, 8))),
        "w_down": bell_draw(seeds[13], (FF, D), FF ** -0.5, 0.046875, ((0, 8), (1, 2))),
    }


NEG_FILL = -1e+30
EPSILON = 1e-05
LOG2E = 1.4426950408889634

def reference(queries, fresh_keys, fresh_values, residual_in, cache_keys, cache_values, key_scales, value_scales, page_table, row_lengths, norm_gain, w_gate, w_up, w_down):
    heads_per = H // KVH
    inv_root = LOG2E / math.sqrt(HD)
    cache_index = jnp.arange(CACHE, dtype=jnp.int32)
    device_of = (cache_index // CACHE_DEV).astype(jnp.int32)
    slot_block = (cache_index % CACHE_DEV // BLK).astype(jnp.int32)
    logical = device_of * BPD + page_table[device_of, slot_block].astype(jnp.int32)
    position = logical * BLK + cache_index % BLK
    visible = position[None, :] < row_lengths[:, None]
    k_scale = jnp.repeat(key_scales, BLK, axis=1)
    v_scale = jnp.repeat(value_scales, BLK, axis=1)
    fresh_k = jnp.moveaxis(fresh_keys.reshape(ROWS, STEPS, KVH, HD), 2, 0).astype(jnp.float32)
    fresh_v = jnp.moveaxis(fresh_values.reshape(ROWS, STEPS, KVH, HD), 2, 0).astype(jnp.float32)
    results = []
    for step_index in range(STEPS):
        q_step = jnp.moveaxis(queries[:, step_index].reshape(ROWS, KVH, heads_per, HD), 1, 0).astype(jnp.float32)
        allowed = jnp.arange(STEPS) <= step_index

        def per_group(operands):
            q_group, key_block, value_block, k_row, v_row, fk_group, fv_group = operands
            raw_scores = jnp.einsum('rqd,cd->rqc', q_group, key_block.astype(jnp.float32), precision=lax.Precision.HIGHEST)
            scores = raw_scores * k_row * inv_root
            fresh_scores = jnp.einsum('rqd,rtd->rqt', q_group, fk_group, precision=lax.Precision.HIGHEST) * inv_root
            cache_mask = visible[:, None, :]
            fresh_mask = allowed[None, None, :]
            row_top = jnp.maximum(lax.optimization_barrier(jnp.max(jnp.where(cache_mask, scores, NEG_FILL), axis=-1)), lax.optimization_barrier(jnp.max(jnp.where(fresh_mask, fresh_scores, NEG_FILL), axis=-1)))
            row_top = jnp.ceil(row_top)
            cache_terms = jnp.where(cache_mask, jnp.exp2(scores - row_top[..., None]), 0.0)
            fresh_terms = jnp.where(fresh_mask, jnp.exp2(fresh_scores - row_top[..., None]), 0.0)
            row_total = lax.optimization_barrier(jnp.sum(cache_terms, axis=-1)) + lax.optimization_barrier(jnp.sum(fresh_terms, axis=-1))
            cache_weights = lax.optimization_barrier((cache_terms * v_row).astype(jnp.bfloat16)).astype(jnp.float32)
            fresh_weights = lax.optimization_barrier(fresh_terms.astype(jnp.bfloat16)).astype(jnp.float32)
            weighted = jnp.einsum('rqc,cd->rqd', cache_weights, value_block.astype(jnp.float32), precision=lax.Precision.HIGHEST)
            weighted = weighted + jnp.einsum('rqt,rtd->rqd', fresh_weights, fv_group, precision=lax.Precision.HIGHEST)
            return weighted / row_total[..., None]
        attention = lax.map(per_group, (q_step, cache_keys, cache_values, k_scale, v_scale, fresh_k, fresh_v))
        attention = jnp.moveaxis(attention, 0, 1).reshape(ROWS, D)
        hidden_state = residual_in[:, step_index].astype(jnp.float32) + attention
        inverse_rms = lax.rsqrt(lax.optimization_barrier(jnp.sum(hidden_state * hidden_state, axis=-1)) / D + EPSILON)
        normed = (hidden_state * inverse_rms[:, None] * norm_gain).astype(jnp.bfloat16)
        gate_sums = jnp.dot(normed, w_gate, preferred_element_type=jnp.float32)
        up_sums = jnp.dot(normed, w_up, preferred_element_type=jnp.float32)
        hidden = (jax.nn.silu(gate_sums) * up_sums).astype(jnp.bfloat16)
        down_sums = jnp.dot(hidden, w_down, preferred_element_type=jnp.float32)
        results.append((hidden_state + down_sums).astype(jnp.bfloat16))
    return jnp.stack(results, axis=1)
```

```python
import functools
import math

import jax
import jax.numpy as jnp
from jax import lax
from jax.experimental import pallas as pl
from jax.experimental.pallas import tpu as pltpu
from jax.sharding import PartitionSpec as P

NEG_FILL = -1e30
TOP_FLOOR = -1e29
EPSILON = 1e-05
LOG2E = 1.4426950408889634
BF = jnp.bfloat16
F32 = jnp.float32
META = 8


def split3(x):
    hi = lax.reduce_precision(x, 8, 7)
    mid = lax.reduce_precision(x - hi, 8, 7)
    return hi, mid, x - hi - mid


def round_up(x, m):
    return (x + m - 1) // m * m


def attention_kernel(
    dims, b_ref, lens_ref, *refs
):
    hs, n, span, pages, rows, tl, steps = dims
    blocks = refs[:hs]
    crosses = refs[hs : hs + n - hs]
    order_ref, acc_ref, stat_ref, send_ref, qs, ks, vs, fk, fv = refs[n:]
    hd = ks.shape[1]
    blk = span // pages
    nq = qs.shape[0]
    q_at = 2 * span + META * pages
    half = b_ref[0]
    for d in range(hs):
        slot = order_ref[d]
        start = pl.multiple_of(slot * rows, rows)
        qs[pl.ds(start, rows), :] = blocks[d][q_at : q_at + rows, :]
        ks[d * span : (d + 1) * span, :] = blocks[d][0:span, :]
        vs[d * span : (d + 1) * span, :] = blocks[d][span : 2 * span, :]
    for d in range(n - hs):
        start = pl.multiple_of(order_ref[hs + d] * rows, rows)
        qs[pl.ds(start, rows), :] = crosses[d][...]
    f_at = q_at + 2 * rows
    fresh = fk.shape[0] // hs
    for d in range(hs):
        fk[d * fresh : (d + 1) * fresh, :] = blocks[d][f_at : f_at + fresh, :]
        fv[d * fresh : (d + 1) * fresh, :] = blocks[d][f_at + fresh : f_at + 2 * fresh, :]
    lanes = min(256, nq)
    inv_root = LOG2E / math.sqrt(hd)

    def chunk(c, carry):
        at = pl.multiple_of(c * lanes, lanes)
        q = qs[pl.ds(at, lanes), :]
        length = lens_ref[0:1, pl.ds(at, lanes)]
        dims_nt = (((1,), (1,)), ((), ()))
        raw = lax.dot_general(ks[...], q, dims_nt, preferred_element_type=F32)
        inner = lax.broadcasted_iota(jnp.int32, (blk, lanes), 0).astype(F32)
        scores = []
        v_rows = []
        for d in range(hs):
            meta = blocks[d][2 * span : 2 * span + META * pages, :].astype(F32)
            for page in range(pages):
                at_meta = page * META
                k_scale = (
                    meta[at_meta : at_meta + 1, 0:1]
                    + meta[at_meta + 1 : at_meta + 2, 0:1]
                    + meta[at_meta + 2 : at_meta + 3, 0:1]
                )
                v_scale = (
                    meta[at_meta + 3 : at_meta + 4, 0:1]
                    + meta[at_meta + 4 : at_meta + 5, 0:1]
                    + meta[at_meta + 5 : at_meta + 6, 0:1]
                )
                first = meta[at_meta + 6 : at_meta + 7, 0:1] * float(blk)
                base = d * span + page * blk
                limit = length - first
                part = raw[base : base + blk, :] * (k_scale * inv_root)
                scores.append(jnp.where(inner < limit, part, NEG_FILL))
                v_rows.append(v_scale)
        lane = lax.broadcasted_iota(jnp.int32, (1, lanes), 1) + at
        source = lane // rows
        token = lane % tl
        fi = lax.broadcasted_iota(jnp.int32, (fk.shape[0], lanes), 0)
        f_slot = fi // fresh
        f_token = fi % fresh
        same = jnp.zeros((fk.shape[0], lanes), jnp.bool_)
        for d in range(hs):
            same = same | ((f_slot == d) & (source == order_ref[d]))
        keep = same & (f_token // steps == token // steps) & (f_token % steps <= token % steps)
        keep = keep & (f_token < tl)
        raw_f = lax.dot_general(fk[...], q, dims_nt, preferred_element_type=F32) * inv_root
        fresh_scores = jnp.where(keep, raw_f, NEG_FILL)
        top = jnp.max(fresh_scores, axis=0, keepdims=True)
        for part in scores:
            top = jnp.maximum(top, jnp.max(part, axis=0, keepdims=True))
        top = jnp.maximum(jnp.ceil(top), TOP_FLOOR)
        fresh_terms = jnp.exp2(fresh_scores - top)
        total = jnp.sum(fresh_terms, axis=0, keepdims=True)
        weights = []
        for part, v_scale in zip(scores, v_rows):
            terms = jnp.exp2(part - top)
            total = total + jnp.sum(terms, axis=0, keepdims=True)
            weights.append((terms * v_scale).astype(BF))
        weight = jnp.concatenate(weights, axis=0)
        dims_tn = (((0,), (0,)), ((), ()))
        acc = lax.dot_general(vs[...], weight, dims_tn, preferred_element_type=F32)
        acc = acc + lax.dot_general(fv[...], fresh_terms.astype(BF), dims_tn, preferred_element_type=F32)
        acc_ref[:, pl.ds(at, lanes)] = acc
        send_ref[0:hd, pl.ds(at, lanes)] = acc.astype(BF)
        zero = jnp.zeros((1, lanes), F32)
        stat_ref[:, pl.ds(at, lanes)] = jnp.concatenate([top, total] + [zero] * 6, axis=0)
        pieces = []
        for value in (top, total):
            hi = value.astype(BF).astype(F32)
            mid = (value - hi).astype(BF).astype(F32)
            pieces += [hi, mid, value - hi - mid]
        pieces += [zero] * 10
        send_ref[hd : hd + 16, pl.ds(at, lanes)] = jnp.concatenate(pieces, axis=0).astype(BF)
        return carry

    lax.fori_loop(0, nq // lanes, chunk, 0)


def combine_kernel(dims, order_ref, acc_ref, stat_ref, gain_ref, *refs):
    hs, r, rows, tl, aligned, res_at = dims
    n = hs * r
    received = refs[: r - 1]
    blocks = refs[r - 1 : r - 1 + hs]
    residuals = refs[r - 1 + hs : 2 * (r - 1) + hs]
    out_ref, mixed = refs[2 * (r - 1) + hs :]
    hd = acc_ref.shape[0]
    hp = rows // tl
    top = stat_ref[0:1, :]
    total = stat_ref[1:2, :]
    others = []
    for ref in received:
        stats = ref[hd : hd + 16, :].astype(F32)
        o_top = stats[0:1, :] + stats[1:2, :] + stats[2:3, :]
        o_total = stats[3:4, :] + stats[4:5, :] + stats[5:6, :]
        others.append((o_top, o_total, ref))
    best = top
    for o_top, _, _ in others:
        best = jnp.maximum(best, o_top)
    factor = jnp.exp2(top - best)
    total = total * factor
    for o_top, o_total, _ in others:
        total = total + o_total * jnp.exp2(o_top - best)
    value = acc_ref[...] * (factor / total)
    for o_top, _, ref in others:
        value = value + ref[0:hd, :].astype(F32) * (jnp.exp2(o_top - best) / total)
    mixed[...] = value
    gain = gain_ref[...]
    for d in range(n):
        source = order_ref[d]
        start = pl.multiple_of(source * rows, rows)
        if rows % 128 == 0:
            part = mixed[:, pl.ds(start, rows)].T
        else:
            part = jnp.zeros((hd, rows), F32)
            for s in range(n):
                part = part + jnp.where(source == s, mixed[:, s * rows : (s + 1) * rows], 0.0)
            part = part.T
        if d < hs:
            res = blocks[d][res_at : res_at + rows, :]
        else:
            which, da = divmod(d - hs, hs)
            res = residuals[which][da * rows : (da + 1) * rows, :]
        part = ((part + res.astype(F32)) * gain).astype(BF)
        slot = lax.rem(source, hs) * r + source // hs
        if aligned:
            at = pl.multiple_of(slot * tl, tl)
            for h in range(hp):
                out_ref[pl.ds(at, tl), h * hd : (h + 1) * hd] = part[h * tl : (h + 1) * tl, :]
        else:
            out_ref[slot] = part


def gate_up_kernel(first, last, ffp, index_ref, p_ref, gain_ref, wg_ref, wu_ref, *refs):
    tile = wg_ref.shape[1]
    step = pl.program_id(0)
    if first:
        outs = refs
    else:
        g_in, u_in, s_in = refs[:3]
        outs = refs[3:]
    g_out, u_out, s_out = outs[:3]
    p = p_ref[...]
    gate = jnp.dot(p, wg_ref[...], preferred_element_type=F32)
    up = jnp.dot(p, wu_ref[...], preferred_element_type=F32)
    if not first:
        gate = gate + g_in[...]
        up = up + u_in[...]
    g_out[...] = gate
    u_out[...] = up

    @pl.when(step == 0)
    def _():
        ssq = jnp.zeros(s_out.shape, F32) if first else s_in[...]
        hd = s_out.shape[1]
        for k in range(p_ref.shape[1] // hd):
            h = p_ref[:, k * hd : (k + 1) * hd].astype(F32) / gain_ref[:, k * hd : (k + 1) * hd]
            ssq = ssq + h * h
        s_out[...] = ssq


def gate_up(first, index, p, gain, w_gate, w_up, tile, carry):
    tokens, width = p.shape
    ffl = w_gate.shape[1]
    tiles = ffl // tile
    fixed = lambda i, s: (0, 0)
    in_specs = [
        pl.BlockSpec((tokens, width), fixed),
        pl.BlockSpec((1, width), lambda i, s: (0, s[0])),
        pl.BlockSpec((width, tile), lambda i, s: (s[0], i)),
        pl.BlockSpec((width, tile), lambda i, s: (s[0], i)),
    ]
    col = pl.BlockSpec((tokens, tile), lambda i, s: (0, i))
    stat = pl.BlockSpec((tokens, 128), fixed)
    args = [p, gain, w_gate, w_up]
    if not first:
        in_specs += [col, col, stat]
        args += list(carry)
    out_shape = (
        jax.ShapeDtypeStruct((tokens, ffl), F32),
        jax.ShapeDtypeStruct((tokens, ffl), F32),
        jax.ShapeDtypeStruct((tokens, 128), F32),
    )
    return pl.pallas_call(
        functools.partial(gate_up_kernel, first, False, 0),
        out_shape=out_shape,
        grid_spec=pltpu.PrefetchScalarGridSpec(
            num_scalar_prefetch=1,
            grid=(tiles,),
            in_specs=in_specs,
            out_specs=(col, col, stat),
        ),
        compiler_params=pltpu.CompilerParams(vmem_limit_bytes=24 << 20),
        cost_estimate=pl.CostEstimate(
            flops=4 * tokens * width * ffl, bytes_accessed=4 * width * ffl, transcendentals=0
        ),
    )(index, *args)


def down_kernel(hs, index_ref, hid_ref, wd_ref, *outs):
    value = jnp.dot(hid_ref[...], wd_ref[...], preferred_element_type=F32)
    scratch = outs[-1]
    scratch[...] = value
    per = value.shape[0] // hs
    for d in range(hs):
        at = pl.multiple_of(index_ref[d] * per, per)
        outs[d][...] = scratch[pl.ds(at, per), :].astype(outs[d].dtype)


def down(hs, index, hidden, w_down, chunk, width):
    tokens, ffl = hidden.shape
    per = tokens // hs
    tile = min(width, 512)
    tiles = width // tile
    offset = chunk * tiles
    out = pl.BlockSpec((per, tile), lambda i, s: (0, i))
    return pl.pallas_call(
        functools.partial(down_kernel, hs),
        out_shape=tuple(
            jax.ShapeDtypeStruct((per, width), F32 if d == 0 else BF) for d in range(hs)
        ),
        grid_spec=pltpu.PrefetchScalarGridSpec(
            num_scalar_prefetch=1,
            grid=(tiles,),
            in_specs=[
                pl.BlockSpec((tokens, ffl), lambda i, s: (0, 0)),
                pl.BlockSpec((ffl, tile), lambda i, s: (0, offset + i)),
            ],
            out_specs=(out,) * hs,
            scratch_shapes=[pltpu.VMEM((tokens, tile), F32)],
        ),
        compiler_params=pltpu.CompilerParams(vmem_limit_bytes=24 << 20),
        cost_estimate=pl.CostEstimate(
            flops=2 * tokens * ffl * width, bytes_accessed=2 * ffl * width, transcendentals=0
        ),
    )(index, hidden, w_down)


def make_body(n):
    def body(
        queries,
        fresh_keys,
        fresh_values,
        residual_in,
        cache_keys,
        cache_values,
        key_scales,
        value_scales,
        page_table,
        row_lengths,
        norm_gain,
        w_gate,
        w_up,
        w_down,
    ):
        rl, steps, half = queries.shape
        kv_heads, span, hd = cache_keys.shape
        pages = page_table.shape[1]
        hp = half // (kv_heads * hd)
        hs = math.gcd(kv_heads, n)
        assert hs == kv_heads and n * pages <= 256
        r = n // hs
        tl = rl * steps
        rows = hp * tl
        nq = n * rows
        tokens = n * tl
        width = hp * hd
        ffl = w_gate.shape[1]
        model = half * 2
        index = lax.axis_index("seq")
        a = lax.rem(index, hs)
        b = index // hs
        pow2 = hs & (hs - 1) == 0

        def mate(x, d):
            return x ^ d if pow2 else (x + d) % hs

        def origin(x, d):
            return x ^ d if pow2 else (x - d) % hs

        def shift(x, db, da):
            pairs = []
            for i in range(n):
                bi, ai = divmod(i, hs)
                pairs.append((i, ((bi + db) % r) * hs + mate(ai, da)))
            return lax.ppermute(x, "seq", pairs)

        targets = [mate(a, d) if pow2 else lax.rem(a + d, hs) for d in range(hs)]
        sources = [origin(a, d) if pow2 else lax.rem(a - d + hs, hs) for d in range(hs)]

        page_id = (index * pages + page_table[0]).astype(F32)
        page_id = jnp.broadcast_to(page_id[None, :], (kv_heads, pages))
        zero = jnp.zeros((kv_heads, pages), F32)
        meta = jnp.stack([*split3(key_scales), *split3(value_scales), page_id, zero], axis=-1)
        meta = jnp.broadcast_to(meta.reshape(kv_heads, pages * META, 1), (kv_heads, pages * META, hd))
        by_head = lambda x: jnp.moveaxis(x.reshape(tl, kv_heads, -1, hd), 0, 2).reshape(kv_heads, -1, hd)
        q_heads = by_head(queries)
        res_heads = by_head(residual_in)
        fk_heads = by_head(fresh_keys)
        fv_heads = by_head(fresh_values)
        fpad = round_up(tl, 16)
        if fpad != tl:
            fk_heads = jnp.pad(fk_heads, ((0, 0), (0, fpad - tl), (0, 0)))
            fv_heads = jnp.pad(fv_heads, ((0, 0), (0, fpad - tl), (0, 0)))
        payload = jnp.concatenate(
            [cache_keys, cache_values, meta.astype(BF), q_heads, res_heads, fk_heads, fv_heads], axis=1
        )
        pick = lambda x, i: lax.dynamic_index_in_dim(x, i, 0, keepdims=False)
        blocks = [pick(payload, a)]
        for d in range(1, hs):
            blocks.append(shift(pick(payload, targets[d]), 0, d))
        order = [b * hs + s for s in sources]
        crosses = []
        for db in range(1, r):
            for d in range(hs):
                crosses.append(shift(pick(q_heads, targets[d]), db, d))
                order.append(lax.rem(b - db + r, r) * hs + sources[d])
        order = jnp.stack(order).astype(jnp.int32)
        lens = jnp.broadcast_to(
            row_lengths.reshape(n, 1, rl, 1).astype(F32), (n, hp, rl, steps)
        ).reshape(1, nq)
        smem = pl.BlockSpec(memory_space=pltpu.SMEM)
        vmem = pl.BlockSpec(memory_space=pltpu.VMEM)
        acc, stat, sent = pl.pallas_call(
            functools.partial(attention_kernel, (hs, n, span, pages, rows, tl, steps)),
            out_shape=(
                jax.ShapeDtypeStruct((hd, nq), F32),
                jax.ShapeDtypeStruct((8, nq), F32),
                jax.ShapeDtypeStruct((hd + 16, nq), BF),
            ),
            in_specs=[smem, vmem] + [vmem] * n + [smem],
            out_specs=(vmem, vmem, vmem),
            scratch_shapes=[
                pltpu.VMEM((nq, hd), BF),
                pltpu.VMEM((hs * span, hd), BF),
                pltpu.VMEM((hs * span, hd), BF),
                pltpu.VMEM((hs * fpad, hd), BF),
                pltpu.VMEM((hs * fpad, hd), BF),
            ],
            compiler_params=pltpu.CompilerParams(vmem_limit_bytes=32 << 20),
            cost_estimate=pl.CostEstimate(
                flops=4 * nq * hs * span * hd, bytes_accessed=4 << 20, transcendentals=nq * hs * span
            ),
        )(b.reshape(1).astype(jnp.int32), lens, *blocks, *crosses, order)
        res_at = 2 * span + META * pages + rows
        own_res = jnp.concatenate([x[res_at : res_at + rows] for x in blocks], axis=0)
        received = [shift(sent, db, 0) for db in range(1, r)]
        residuals = [shift(own_res, db, 0) for db in range(1, r)]
        gain_rows = jnp.broadcast_to(
            norm_gain.reshape(kv_heads, hp, 1, hd), (kv_heads, hp, tl, hd)
        ).reshape(kv_heads, rows, hd)
        aligned = tl % 16 == 0
        p_shape = (tokens, width) if aligned else (n, rows, hd)
        p = pl.pallas_call(
            functools.partial(combine_kernel, (hs, r, rows, tl, aligned, res_at)),
            out_shape=jax.ShapeDtypeStruct(p_shape, BF),
            in_specs=[smem] + [vmem] * (3 + 2 * (r - 1) + hs),
            out_specs=vmem,
            scratch_shapes=[pltpu.VMEM((hd, nq), F32)],
            compiler_params=pltpu.CompilerParams(vmem_limit_bytes=(32 if aligned else 60) << 20),
        )(order, acc, stat, pick(gain_rows, a), *received, *blocks, *residuals)
        if not aligned:
            p = jnp.moveaxis(p.reshape(n, hp, tl, hd), 1, 2).reshape(tokens, width)
        parts = [p] + [shift(p, 0, d) for d in range(1, hs)]
        gain2 = norm_gain.reshape(1, half)
        tile = 256 if ffl % 256 == 0 else ffl
        carry = None
        for d in range(hs):
            carry = gate_up(
                d == 0, sources[d].reshape(1).astype(jnp.int32), parts[d], gain2, w_gate, w_up, tile, carry
            )
        gate_part, up_part, ssq_part = carry
        ssq_sum = jnp.sum(ssq_part, axis=-1, keepdims=True)
        hi, mid, lo = split3(ssq_sum)
        message = jnp.concatenate(
            [gate_part, up_part, hi, mid, lo], axis=1
        ).astype(BF)
        other = lax.ppermute(message, "tensor", [(0, 1), (1, 0)]).astype(F32)
        square = ssq_sum + (
            other[:, 2 * ffl : 2 * ffl + 1]
            + other[:, 2 * ffl + 1 : 2 * ffl + 2]
            + other[:, 2 * ffl + 2 : 2 * ffl + 3]
        )
        inverse = lax.rsqrt(square / model + EPSILON)
        gate = (gate_part + other[:, :ffl]) * inverse
        up = (up_part + other[:, ffl : 2 * ffl]) * inverse
        hidden = (jax.nn.silu(gate) * up).astype(BF)

        slot = a * r + b
        own = [lax.dynamic_slice_in_dim(x, slot * tl, tl, 0).astype(F32) for x in parts]
        own = [
            x / lax.dynamic_slice_in_dim(norm_gain, s * width, width, 0)[None, :]
            for x, s in zip(own, sources)
        ]
        state = jnp.stack(own)
        blocks_abs = []
        for i in range(hs):
            pickd = jnp.zeros_like(own[0])
            for d in range(hs):
                pickd = pickd + jnp.where(sources[d] == i, own[d], 0.0)
            blocks_abs.append(pickd)
        state = jnp.concatenate(blocks_abs, axis=1)
        chunks = 4
        cw = half // chunks
        target_index = jnp.stack(targets).astype(jnp.int32)
        outs = []
        for c in range(chunks):
            pieces = down(hs, target_index, hidden, w_down, c, cw)
            got = [shift(pieces[d], 0, d) for d in range(1, hs)]
            total = pieces[0]
            for x in got:
                total = total + x.astype(F32)
            total = total.reshape(r, tl, cw)
            mine = lax.dynamic_index_in_dim(total, b, 0, keepdims=False)
            for db in range(1, r):
                away = lax.dynamic_index_in_dim(total, lax.rem(b + db, r), 0, keepdims=False)
                mine = mine + shift(away.astype(BF), db, 0).astype(F32)
            outs.append((state[:, c * cw : (c + 1) * cw] + mine).astype(BF))
        return jnp.concatenate(outs, axis=1).reshape(rl, steps, half)

    return body


def solution(mesh):
    in_specs = (
        P(("groups", "seq"), None, "tensor"),
        P(("groups", "seq"), None, "tensor"),
        P(("groups", "seq"), None, "tensor"),
        P(("groups", "seq"), None, "tensor"),
        P("tensor", ("groups", "seq"), None),
        P("tensor", ("groups", "seq"), None),
        P("tensor", ("groups", "seq")),
        P("tensor", ("groups", "seq")),
        P(("groups", "seq"), None),
        P("groups"),
        P("tensor"),
        P("tensor", "seq"),
        P("tensor", "seq"),
        P("seq", "tensor"),
    )
    out_specs = P(("groups", "seq"), None, "tensor")
    body = make_body(mesh.shape["seq"])
    return jax.shard_map(body, mesh=mesh, in_specs=in_specs, out_specs=out_specs, check_vma=False)
```

```python
import functools
import math

import jax
import jax.numpy as jnp
from jax import lax
from jax.experimental import pallas as pl
from jax.experimental.pallas import tpu as pltpu
from jax.sharding import PartitionSpec as P


NEG_FILL = -1e30
TOP_FLOOR = -1e29
EPSILON = 1e-05
LOG2E = 1.4426950408889634
BF = jnp.bfloat16
F32 = jnp.float32
META = 8


def split3(x):
    hi = lax.reduce_precision(x, 8, 7)
    mid = lax.reduce_precision(x - hi, 8, 7)
    return hi, mid, x - hi - mid


def round_up(x, m):
    return (x + m - 1) // m * m


VMEM = pl.BlockSpec(memory_space=pltpu.VMEM)
SMEM = pl.BlockSpec(memory_space=pltpu.SMEM)
HBM = pl.BlockSpec(memory_space=pltpu.HBM)
NT = (((1,), (1,)), ((), ()))
TN = (((0,), (0,)), ((), ()))


def hbm(x):
    return pltpu.with_memory_space_constraint(x, pltpu.HBM)


def resident(x):
    return pltpu.with_memory_space_constraint(x, pltpu.VMEM)


def params(mib):
    return pltpu.CompilerParams(vmem_limit_bytes=mib << 20)


def pack_kernel(dims, scal, k_scale, v_scale, pages_ref, q_ref, res_ref, fk_ref, fv_ref, k_ref, v_ref, *refs):
    hs, n, span, pages, rows, tl = dims
    outs, crosses, sems = refs[:hs], refs[hs : 2 * hs], refs[2 * hs]
    hd = k_ref.shape[2]
    hp = rows // tl
    copies = []
    for d in range(hs):
        target = scal[n + d]
        for j, ref in enumerate((k_ref, v_ref)):
            copy = pltpu.make_async_copy(ref.at[target], outs[d].at[pl.ds(j * span, span)], sems.at[d, j])
            copy.start()
            copies.append(copy)
    index = scal[n + hs]
    q_at = 2 * span + META * pages
    row = lax.broadcasted_iota(jnp.int32, (META, hd), 0)
    for d in range(hs):
        target = scal[n + d]
        tiles = []
        for page in range(pages):
            page_id = (index * pages + pages_ref[0, page]).astype(F32)
            value = jnp.where(row < 3, k_scale[target, page], jnp.where(row < 6, v_scale[target, page], page_id))
            hi = value.astype(BF).astype(F32)
            mid = (value - hi).astype(BF).astype(F32)
            low = value - hi - mid
            first = (row == 0) | (row == 3) | (row >= 6)
            second = (row == 1) | (row == 4)
            tiles.append(jnp.where(first, hi, jnp.where(second, mid, low)))
        for pair in range(pages // 2):
            at = 2 * span + pair * 2 * META
            both = jnp.concatenate([tiles[2 * pair], tiles[2 * pair + 1]], axis=0)
            outs[d][at : at + 2 * META, :] = both.astype(BF)
        for h in range(hp):
            at = pl.multiple_of(target * (hp * hd) + h * hd, hd)
            q = q_ref[:, :, pl.ds(at, hd)].reshape(tl, hd)
            res = res_ref[:, :, pl.ds(at, hd)].reshape(tl, hd)
            outs[d][q_at + h * tl : q_at + (h + 1) * tl, :] = q
            outs[d][q_at + rows + h * tl : q_at + rows + (h + 1) * tl, :] = res
            crosses[d][h * tl : (h + 1) * tl, :] = q
            crosses[d][rows + h * tl : rows + (h + 1) * tl, :] = res
        at = pl.multiple_of(target * hd, hd)
        f_at = q_at + 2 * rows
        outs[d][f_at : f_at + tl, :] = fk_ref[:, :, pl.ds(at, hd)].reshape(tl, hd)
        outs[d][f_at + tl : f_at + 2 * tl, :] = fv_ref[:, :, pl.ds(at, hd)].reshape(tl, hd)
    for copy in copies:
        copy.wait()


def attention_kernel(dims, scal, row_len, *refs):
    hs, n, span, pages, rows, tl, steps, first_source, count = dims
    blocks = refs[:hs]
    crosses = refs[hs:n]
    acc_ref, stat_ref, send_ref, qs, ks, vs, fk, fv, scale, lens_ref = refs[n:]
    hd = ks.shape[1]
    blk = span // pages
    nq = count * rows
    q_at = 2 * span + META * pages
    inv_root = LOG2E / math.sqrt(hd)
    for d in range(n):
        ref, at = (blocks[d], q_at) if d < hs else (crosses[d - hs], 0)
        start = pl.multiple_of(scal[d] * rows, rows)
        qs[pl.ds(start, rows), :] = ref[at : at + rows, :]
    f_at = q_at + 2 * rows
    fresh = fk.shape[0] // hs
    for d in range(hs):
        ks[d * span : (d + 1) * span, :] = blocks[d][0:span, :]
        vs[d * span : (d + 1) * span, :] = blocks[d][span : 2 * span, :]
        fk[d * fresh : (d + 1) * fresh, :] = blocks[d][f_at : f_at + fresh, :]
        fv[d * fresh : (d + 1) * fresh, :] = blocks[d][f_at + fresh : f_at + 2 * fresh, :]
        meta = blocks[d][2 * span : 2 * span + META * pages, :].astype(F32)
        for page in range(pages):
            m = meta[page * META : (page + 1) * META, :]
            k_row = (m[0:1] + m[1:2] + m[2:3]) * inv_root
            v_row = m[3:4] + m[4:5] + m[5:6]
            at = (d * pages + page) * META
            scale[at : at + META, :] = jnp.concatenate([k_row, v_row, m[6:7] * float(blk), m[3:8]], axis=0)
    lanes = min(256, nq)
    base_q = first_source * rows
    lane = lax.broadcasted_iota(jnp.int32, (1, nq), 1)
    rl = tl // steps
    lane_row = (lane // rows) * rl + (lane % tl) // steps
    lens = jnp.zeros((1, nq), F32)
    for j in range(count * rl):
        lens = jnp.where(lane_row == j, row_len[first_source * rl + j].astype(F32), lens)
    lens_ref[...] = lens

    def chunk(c, carry):
        at = pl.multiple_of(c * lanes, lanes)
        at_q = pl.multiple_of(base_q + c * lanes, lanes)
        q = qs[pl.ds(at_q, lanes), :]
        length = lens_ref[0:1, pl.ds(at, lanes)]
        raw = lax.dot_general(ks[...], q, NT, preferred_element_type=F32)
        inner = lax.broadcasted_iota(jnp.int32, (blk, lanes), 0).astype(F32)
        scores = []
        for page in range(hs * pages):
            k_scale = scale[page * META : page * META + 1, 0:1]
            limit = length - scale[page * META + 2 : page * META + 3, 0:1]
            part = raw[page * blk : (page + 1) * blk, :] * k_scale
            scores.append(jnp.where(inner < limit, part, NEG_FILL))
        lane = lax.broadcasted_iota(jnp.int32, (1, lanes), 1) + at_q
        source = lane // rows
        token = lane % tl
        fi = lax.broadcasted_iota(jnp.int32, (fk.shape[0], 1), 0)
        f_slot = fi // fresh
        f_token = fi % fresh
        f_source = jnp.where(f_token < tl, scal[0], -1)
        for d in range(1, hs):
            f_source = jnp.where((f_slot == d) & (f_token < tl), scal[d], f_source)
        keep = (f_source == source) & (f_token // steps == token // steps) & (f_token % steps <= token % steps)
        raw_f = lax.dot_general(fk[...], q, NT, preferred_element_type=F32) * inv_root
        fresh_scores = jnp.where(keep, raw_f, NEG_FILL)
        top = jnp.max(fresh_scores, axis=0, keepdims=True)
        for part in scores:
            top = jnp.maximum(top, jnp.max(part, axis=0, keepdims=True))
        top = jnp.maximum(jnp.ceil(top), TOP_FLOOR)
        fresh_terms = jnp.exp2(fresh_scores - top)
        total = jnp.sum(fresh_terms, axis=0, keepdims=True)
        weights = []
        for page, part in enumerate(scores):
            terms = jnp.exp2(part - top)
            total = total + jnp.sum(terms, axis=0, keepdims=True)
            weights.append((terms * scale[page * META + 1 : page * META + 2, 0:1]).astype(BF))
        weight = jnp.concatenate(weights, axis=0)
        acc = lax.dot_general(vs[...], weight, TN, preferred_element_type=F32)
        acc = acc + lax.dot_general(fv[...], fresh_terms.astype(BF), TN, preferred_element_type=F32)
        acc_ref[:, pl.ds(at, lanes)] = acc
        send_ref[0:hd, pl.ds(at, lanes)] = acc.astype(BF)
        zero = jnp.zeros((1, lanes), F32)
        stat_ref[:, pl.ds(at, lanes)] = jnp.concatenate([top, total] + [zero] * 6, axis=0)
        pieces = []
        for value in (top, total):
            hi = value.astype(BF).astype(F32)
            mid = (value - hi).astype(BF).astype(F32)
            pieces += [hi, mid, value - hi - mid]
        pieces += [zero] * 10
        send_ref[hd : hd + 16, pl.ds(at, lanes)] = jnp.concatenate(pieces, axis=0).astype(BF)
        return carry

    lax.fori_loop(0, nq // lanes, chunk, 0)


def combine_kernel(dims, scal, acc_ref, stat_ref, gain_ref, *refs):
    hs, r, rows, tl, aligned, res_at, first_source, count = dims
    n = hs * r
    received = refs[: r - 1]
    blocks = refs[r - 1 : r - 1 + hs]
    crosses = refs[r - 1 + hs : r - 1 + n]
    out_ref, res = refs[r - 1 + n :]
    hd = acc_ref.shape[0]
    hp = rows // tl
    per = count // hs
    for d in range(n):
        ref, at = (blocks[d], res_at) if d < hs else (crosses[d - hs], rows)
        start = pl.multiple_of(scal[d] * rows, rows)
        res[pl.ds(start, rows), :] = ref[at : at + rows, :]
    top = stat_ref[0:1, :]
    total = stat_ref[1:2, :]
    others = []
    for ref in received:
        stats = ref[hd : hd + 16, :].astype(F32)
        o_top = stats[0:1, :] + stats[1:2, :] + stats[2:3, :]
        o_total = stats[3:4, :] + stats[4:5, :] + stats[5:6, :]
        others.append((o_top, o_total, ref))
    best = top
    for o_top, _, _ in others:
        best = jnp.maximum(best, o_top)
    factor = jnp.exp2(top - best)
    total = total * factor
    for o_top, o_total, _ in others:
        total = total + o_total * jnp.exp2(o_top - best)
    value = acc_ref[...] * (factor / total)
    for o_top, _, ref in others:
        value = value + ref[0:hd, :].astype(F32) * (jnp.exp2(o_top - best) / total)
    width = hp * hd
    gain = gain_ref[0:1, pl.ds(pl.multiple_of(lax.rem(scal[0], hs) * width, width), width)]
    for s in range(count):
        part = value[:, s * rows : (s + 1) * rows].T
        at = (first_source + s) * rows
        part = part + res[at : at + rows, :].astype(F32)
        slot = (s % hs) * per + s // hs
        heads = [part[h * tl : (h + 1) * tl, :] * gain[:, h * hd : (h + 1) * hd] for h in range(hp)]
        if aligned:
            for h in range(hp):
                out_ref[slot * tl : (slot + 1) * tl, h * hd : (h + 1) * hd] = heads[h].astype(BF)
        else:
            out_ref[slot] = jnp.concatenate(heads, axis=0).astype(BF)


def prefetch_kernel(count, pieces, *refs):
    ins, outs, sems = refs[:count], refs[count : 2 * count], refs[2 * count]
    copies = []
    for j in range(count):
        step = ins[j].shape[0] // pieces
        for c in range(pieces):
            at = pl.ds(c * step, step)
            copy = pltpu.make_async_copy(ins[j].at[at], outs[j].at[at], sems.at[j, c])
            copy.start()
            copies.append(copy)
    for copy in copies:
        copy.wait()


def prefetch(*arrays):
    count = len(arrays)
    pieces = 4
    return pl.pallas_call(
        functools.partial(prefetch_kernel, count, pieces),
        out_shape=[pltpu.VMEM(x.shape, x.dtype) for x in arrays],
        in_specs=[HBM] * count,
        out_specs=[VMEM] * count,
        scratch_shapes=[pltpu.SemaphoreType.DMA((count, pieces))],
        compiler_params=params(1),
    )(*[hbm(x) for x in arrays])


def gate_up_kernel(dims, scal, *refs):
    first, offsets, halves, ffl, tile = dims
    if first:
        state = ()
    else:
        state, refs = refs[:2], refs[2:]
    parts = refs[: len(offsets) * halves]
    gain_ref, wg_ref, wu_ref = refs[len(parts) : len(parts) + 3]
    outs = refs[len(parts) + 3 :]
    p_all = outs[-1]
    out_ref, ssq_ref = outs[0], outs[1]
    per, width = parts[0].shape
    hs = wg_ref.shape[0] // width
    ffp = out_ref.shape[1] // 2
    starts = [pl.multiple_of(lax.rem(scal[d], hs) * width, width) for d in offsets]
    for k in range(len(offsets)):
        for j in range(halves):
            p_all[k, j * per : (j + 1) * per, :] = parts[k * halves + j][...]

    def column(at, size):
        for base, w_ref in ((0, wg_ref), (ffp, wu_ref)):
            value = None if first else state[0][:, pl.ds(base + at, size)]
            for k, start in enumerate(starts):
                term = jnp.dot(
                    p_all[k], w_ref[pl.ds(start, width), pl.ds(at, size)], preferred_element_type=F32
                )
                value = term if value is None else value + term
            out_ref[:, pl.ds(base + at, size)] = value
            if not first:
                outs[2][:, pl.ds(base + at, size)] = value.astype(BF)

    if tile == ffl:
        column(0, ffl)
    else:

        def step(i, carry):
            column(pl.multiple_of(i * tile, tile), tile)
            return carry

        lax.fori_loop(0, ffl // tile, step, 0)
    lanes = ssq_ref.shape[1]
    ssq = jnp.zeros(ssq_ref.shape, F32) if first else state[1][...]
    for k, start in enumerate(starts):
        inverse = 1.0 / gain_ref[0:1, pl.ds(start, width)]
        for c in range(width // lanes):
            cols = slice(c * lanes, (c + 1) * lanes)
            h = p_all[k, :, cols].astype(F32) * inverse[:, cols]
            ssq = ssq + h * h
    if first:
        ssq_ref[...] = ssq
    else:
        total = jnp.sum(ssq, axis=1, keepdims=True) + jnp.zeros(ssq_ref.shape, F32)
        ssq_ref[...] = total
        hi = total.astype(BF).astype(F32)
        mid = (total - hi).astype(BF).astype(F32)
        lane = lax.broadcasted_iota(jnp.int32, total.shape, 1)
        stat = jnp.where(lane == 0, hi, jnp.where(lane == 1, mid, total - hi - mid))
        outs[2][:, 2 * ffp : 2 * ffp + lanes] = stat.astype(BF)


def gate_up(offsets, scal, carry, parts, gain, w_gate, w_up, ffp):
    halves = len(parts) // len(offsets)
    per, width = parts[0].shape
    tokens = per * halves
    ffl = w_gate.shape[1]
    first = carry is None
    tile = 256 if ffl % 256 == 0 else ffl
    out_shape = [
        jax.ShapeDtypeStruct((tokens, 2 * ffp), F32),
        jax.ShapeDtypeStruct((tokens, 128), F32),
    ]
    if not first:
        out_shape.append(jax.ShapeDtypeStruct((tokens, 2 * ffp + 128), BF))
    args = [] if first else list(carry)
    args += list(parts) + [gain, resident(w_gate), resident(w_up)]
    return pl.pallas_call(
        functools.partial(gate_up_kernel, (first, offsets, halves, ffl, tile)),
        out_shape=out_shape,
        in_specs=[SMEM] + [VMEM] * len(args),
        out_specs=[VMEM] * len(out_shape),
        scratch_shapes=[pltpu.VMEM((len(offsets), tokens, width), BF)],
        compiler_params=params(4),
    )(scal, *args)


def down_kernel(dims, scal, *refs):
    first, n, hs, groups, ffl, offset, width, model = dims
    if first:
        own, ssq_ref, other, wd_ref = refs[:4]
        hidden, outs = refs[4], refs[5:]
        ffp = own.shape[1] // 2
        stat = other[:, 2 * ffp : 2 * ffp + 128].astype(F32)
        square = ssq_ref[:, 0:1] + (stat[:, 0:1] + stat[:, 1:2] + stat[:, 2:3])
        inverse = lax.rsqrt(square / model + EPSILON)
        gate = (own[:, 0:ffl] + other[:, 0:ffl].astype(F32)) * inverse
        up = (own[:, ffp : ffp + ffl] + other[:, ffp : ffp + ffl].astype(F32)) * inverse
        hidden[...] = (gate / (1.0 + jnp.exp(-gate)) * up).astype(BF)
    else:
        hidden, wd_ref, outs = refs[0], refs[1], refs[2:]
    pieces, scratch = outs[:-1], outs[-1]
    tokens = hidden.shape[0]
    block = tokens // (hs * groups)
    tile = scratch.shape[1]
    for c in range(width // tile):
        scratch[...] = jnp.dot(
            hidden[...], wd_ref[:, offset + c * tile : offset + (c + 1) * tile], preferred_element_type=F32
        )
        for d in range(hs):
            for g in range(groups):
                at = pl.multiple_of(g * (tokens // groups) + scal[n + d] * block, block)
                pieces[d][g * block : (g + 1) * block, c * tile : (c + 1) * tile] = scratch[
                    pl.ds(at, block), :
                ].astype(pieces[d].dtype)


def down(first, n, hs, groups, scal, args, w_down, offset, width, model):
    tokens = args[0].shape[0]
    ffl = w_down.shape[0]
    per = tokens // hs
    tile = min(width, 512)
    out_shape = [jax.ShapeDtypeStruct((tokens, ffl), BF)] if first else []
    out_shape += [jax.ShapeDtypeStruct((per, width), F32 if d == 0 else BF) for d in range(hs)]
    return pl.pallas_call(
        functools.partial(down_kernel, (first, n, hs, groups, ffl, offset, width, model)),
        out_shape=out_shape,
        in_specs=[SMEM] + [VMEM] * (len(args) + 1),
        out_specs=[VMEM] * len(out_shape),
        scratch_shapes=[pltpu.VMEM((tokens, tile), F32)],
        compiler_params=params(4),
    )(scal, *args, resident(w_down))


def own_kernel(dims, scal, gain_ref, *refs):
    n, hs, groups, tl = dims
    parts, out_ref = refs[:-1], refs[-1]
    per, width = parts[0].shape
    index = scal[n + hs]
    a = lax.rem(index, hs)
    b = index // hs
    rc = n // hs // groups
    slot = (b // rc) * (per // tl) + a * rc + lax.rem(b, rc)
    for d in range(hs):
        h = jnp.zeros((tl, width), F32)
        for g in range(groups):
            part = parts[d * groups + g][...].astype(F32)
            for j in range(per // tl):
                take = slot == g * (per // tl) + j
                h = jnp.where(take, part[j * tl : (j + 1) * tl, :], h)
        start = pl.multiple_of(lax.rem(scal[d], hs) * width, width)
        out_ref[:, pl.ds(start, width)] = h / gain_ref[0:1, pl.ds(start, width)]


def own_state(scal, gain, parts, n, hs, groups, tl):
    half = gain.shape[1]
    return pl.pallas_call(
        functools.partial(own_kernel, (n, hs, groups, tl)),
        out_shape=jax.ShapeDtypeStruct((tl, half), F32),
        in_specs=[SMEM] + [VMEM] * (1 + len(parts)),
        out_specs=VMEM,
        compiler_params=params(8),
    )(scal, gain, *parts)


def square_sum_kernel(dims, scal, *refs):
    n, hs, r, tl = dims
    pieces, mine, aways = refs[:hs], refs[hs], refs[hs + 1 :]
    b = scal[n + hs] // hs
    total = pieces[0][...]
    for ref in pieces[1:]:
        total = total + ref[...].astype(F32)
    rows = [total[j * tl : (j + 1) * tl, :] for j in range(r)]
    for db in range(r):
        want = lax.rem(b + db, r)
        value = rows[0]
        for j in range(1, r):
            value = jnp.where(want == j, rows[j], value)
        if db == 0:
            mine[...] = value
        else:
            aways[db - 1][...] = value.astype(BF)


def square_sum(scal, pieces, n, hs, r, tl):
    width = pieces[0].shape[1]
    return pl.pallas_call(
        functools.partial(square_sum_kernel, (n, hs, r, tl)),
        out_shape=[jax.ShapeDtypeStruct((tl, width), F32)]
        + [jax.ShapeDtypeStruct((tl, width), BF)] * (r - 1),
        in_specs=[SMEM] + [VMEM] * hs,
        out_specs=[VMEM] * r,
        compiler_params=params(8),
    )(scal, *pieces)


def make_body(n):
    def body(
        queries,
        fresh_keys,
        fresh_values,
        residual_in,
        cache_keys,
        cache_values,
        key_scales,
        value_scales,
        page_table,
        row_lengths,
        norm_gain,
        w_gate,
        w_up,
        w_down,
    ):
        rl, steps, half = queries.shape
        kv_heads, span, hd = cache_keys.shape
        pages = page_table.shape[1]
        hp = half // (kv_heads * hd)
        hs = math.gcd(kv_heads, n)
        assert hs == kv_heads and n * pages <= 256
        r = n // hs
        tl = rl * steps
        rows = hp * tl
        nq = n * rows
        width = hp * hd
        ffl = w_gate.shape[1]
        ffp = round_up(ffl, 128)
        model = half * 2
        groups = 2 if r % 2 == 0 else 1
        count = n // groups
        aligned = tl % 16 == 0
        fpad = round_up(tl, 16)
        index = lax.axis_index("seq")
        a = lax.rem(index, hs)
        b = index // hs
        pow2 = hs & (hs - 1) == 0

        def mate(x, d):
            return x ^ d if pow2 else (x + d) % hs

        def origin(x, d):
            return x ^ d if pow2 else (x - d + hs) % hs

        def shift(x, db, da):
            pairs = []
            for i in range(n):
                bi, ai = divmod(i, hs)
                pairs.append((i, ((bi + db) % r) * hs + mate(ai, da)))
            return lax.ppermute(x, "seq", pairs)

        k = jnp.arange(n + hs + 1, dtype=jnp.int32)
        k_source = ((b - k // hs + r) % r) * hs + origin(a, k % hs)
        scal = jnp.where(k < n, k_source, jnp.where(k < n + hs, mate(a, (k - n) % hs), index)).astype(jnp.int32)
        pick = lambda x, i: lax.dynamic_index_in_dim(x, i, 0, keepdims=False)

        length = 2 * span + META * pages + 2 * rows + 2 * fpad
        if aligned:
            packed = pl.pallas_call(
                functools.partial(pack_kernel, (hs, n, span, pages, rows, tl)),
                out_shape=[jax.ShapeDtypeStruct((length, hd), BF)] * hs
                + [jax.ShapeDtypeStruct((2 * rows, hd), BF)] * hs,
                in_specs=[SMEM] * 4 + [VMEM] * 4 + [HBM] * 2,
                out_specs=[VMEM] * (2 * hs),
                scratch_shapes=[pltpu.SemaphoreType.DMA((hs, 2))],
                compiler_params=params(8),
            )(
                scal,
                *[
                    hbm(x)
                    for x in (
                        key_scales,
                        value_scales,
                        page_table,
                        queries,
                        residual_in,
                        fresh_keys,
                        fresh_values,
                        cache_keys,
                        cache_values,
                    )
                ],
            )
            payloads, cross_out = packed[:hs], packed[hs:]
        else:
            page_id = (index * pages + page_table[0]).astype(F32)
            page_id = jnp.broadcast_to(page_id[None, :], (kv_heads, pages))
            zero = jnp.zeros((kv_heads, pages), F32)
            meta = jnp.stack([*split3(key_scales), *split3(value_scales), page_id, zero], axis=-1)
            meta = jnp.broadcast_to(
                meta.reshape(kv_heads, pages * META, 1), (kv_heads, pages * META, hd)
            )
            by_head = lambda x: jnp.moveaxis(x.reshape(tl, kv_heads, -1, hd), 0, 2).reshape(kv_heads, -1, hd)
            pad = ((0, 0), (0, fpad - tl), (0, 0))
            both = jnp.concatenate([by_head(queries), by_head(residual_in)], axis=1)
            payload = jnp.concatenate(
                [
                    cache_keys,
                    cache_values,
                    meta.astype(BF),
                    both,
                    jnp.pad(by_head(fresh_keys), pad),
                    jnp.pad(by_head(fresh_values), pad),
                ],
                axis=1,
            )
            targets = [mate(a, d) for d in range(hs)]
            payloads = [pick(payload, t) for t in targets]
            cross_out = [pick(both, t) for t in targets]
        blocks = [payloads[0]] + [shift(payloads[d], 0, d) for d in range(1, hs)]
        crosses = [shift(cross_out[d], db, d) for db in range(1, r) for d in range(hs)]
        wg, wu = prefetch(w_gate, w_up)
        gain2 = norm_gain.reshape(1, half)
        res_at = 2 * span + META * pages + rows
        nc = count * rows
        partial = []
        for g in range(groups):
            attend = pl.pallas_call(
                functools.partial(
                    attention_kernel, (hs, n, span, pages, rows, tl, steps, g * count, count)
                ),
                out_shape=(
                    jax.ShapeDtypeStruct((hd, nc), F32),
                    jax.ShapeDtypeStruct((8, nc), F32),
                    jax.ShapeDtypeStruct((hd + 16, nc), BF),
                ),
                in_specs=[SMEM, SMEM] + [VMEM] * n,
                out_specs=(VMEM, VMEM, VMEM),
                scratch_shapes=[
                    pltpu.VMEM((nq, hd), BF),
                    pltpu.VMEM((hs * span, hd), BF),
                    pltpu.VMEM((hs * span, hd), BF),
                    pltpu.VMEM((hs * fpad, hd), BF),
                    pltpu.VMEM((hs * fpad, hd), BF),
                    pltpu.VMEM((hs * pages * META, hd), F32),
                    pltpu.VMEM((1, nc), F32),
                ],
                compiler_params=params(8 if aligned else 16),
            )
            acc, stat, sent = attend(scal, hbm(row_lengths), *blocks, *crosses)
            partial.append((acc, stat, [shift(sent, db, 0) for db in range(1, r)]))
        per = count * tl
        mine = []
        for g, (acc, stat, received) in enumerate(partial):
            p_shape = (per, width) if aligned else (count, rows, hd)
            combine = pl.pallas_call(
                functools.partial(combine_kernel, (hs, r, rows, tl, aligned, res_at, g * count, count)),
                out_shape=jax.ShapeDtypeStruct(p_shape, BF),
                in_specs=[SMEM] + [VMEM] * (3 + r - 1 + n),
                out_specs=VMEM,
                scratch_shapes=[pltpu.VMEM((nq, hd), BF)],
                compiler_params=params(6 if aligned else 32),
            )
            p = combine(scal, acc, stat, gain2, *received, *blocks, *crosses)
            if not aligned:
                p = jnp.moveaxis(p.reshape(count, hp, tl, hd), 1, 2).reshape(per, width)
            mine.append(p)
        gathered = [[shift(p, 0, d) for p in mine] for d in range(1, hs)]
        (wd,) = prefetch(w_down)
        carry = gate_up((0,), scal, None, mine, gain2, wg, wu, ffp)
        flat = [p for group in gathered for p in group]
        own, ssq, message = gate_up(tuple(range(1, hs)), scal, carry, flat, gain2, wg, wu, ffp)
        other = lax.ppermute(message, "tensor", [(0, 1), (1, 0)])

        state = own_state(scal, gain2, mine + flat, n, hs, groups, tl)
        chunks = 2
        cw = half // chunks
        sums = []
        args = [own, ssq, other]
        for c in range(chunks):
            pieces = down(c == 0, n, hs, groups, scal, args, wd, c * cw, cw, model)
            if c == 0:
                args, pieces = [pieces[0]], pieces[1:]
            sums.append((pieces[0], [shift(pieces[d], 0, d) for d in range(1, hs)]))
        outs = []
        for c, (total, got) in enumerate(sums):
            result, *aways = square_sum(scal, [total] + got, n, hs, r, tl)
            result = state[:, c * cw : (c + 1) * cw] + result
            for db in range(1, r):
                result = result + shift(aways[db - 1], db, 0).astype(F32)
            outs.append(result.astype(BF))
        return jnp.concatenate(outs, axis=1).reshape(rl, steps, half)

    return body


def solution(mesh):
    in_specs = (
        P(("groups", "seq"), None, "tensor"),
        P(("groups", "seq"), None, "tensor"),
        P(("groups", "seq"), None, "tensor"),
        P(("groups", "seq"), None, "tensor"),
        P("tensor", ("groups", "seq"), None),
        P("tensor", ("groups", "seq"), None),
        P("tensor", ("groups", "seq")),
        P("tensor", ("groups", "seq")),
        P(("groups", "seq"), None),
        P("groups"),
        P("tensor"),
        P("tensor", "seq"),
        P("tensor", "seq"),
        P("seq", "tensor"),
    )
    out_specs = P(("groups", "seq"), None, "tensor")
    body = make_body(mesh.shape["seq"])
    return jax.shard_map(body, mesh=mesh, in_specs=in_specs, out_specs=out_specs, check_vma=False)
```

```python
import functools
import math

import jax
import jax.numpy as jnp
from jax import lax
from jax.experimental import pallas as pl
from jax.experimental.pallas import tpu as pltpu
from jax.sharding import PartitionSpec as P


NEG_FILL = -1e30
TOP_FLOOR = -1e29
EPSILON = 1e-05
LOG2E = 1.4426950408889634
BF = jnp.bfloat16
F32 = jnp.float32
META = 8


def split3(x):
    hi = lax.reduce_precision(x, 8, 7)
    mid = lax.reduce_precision(x - hi, 8, 7)
    return hi, mid, x - hi - mid


def round_up(x, m):
    return (x + m - 1) // m * m


VMEM = pl.BlockSpec(memory_space=pltpu.VMEM)
SMEM = pl.BlockSpec(memory_space=pltpu.SMEM)
HBM = pl.BlockSpec(memory_space=pltpu.HBM)
NT = (((1,), (1,)), ((), ()))
TN = (((0,), (0,)), ((), ()))


def hbm(x):
    return pltpu.with_memory_space_constraint(x, pltpu.HBM)


def resident(x):
    return pltpu.with_memory_space_constraint(x, pltpu.VMEM)


def params(mib):
    return pltpu.CompilerParams(vmem_limit_bytes=mib << 20)


def pack_kernel(dims, scal, k_scale, v_scale, pages_ref, q_ref, res_ref, fk_ref, fv_ref, k_ref, v_ref, *refs):
    hs, n, span, pages, rows, tl = dims
    outs, crosses, sems = refs[:hs], refs[hs : 2 * hs], refs[2 * hs]
    hd = k_ref.shape[2]
    hp = rows // tl
    copies = []
    for d in range(hs):
        target = scal[n + d]
        for j, ref in enumerate((k_ref, v_ref)):
            copy = pltpu.make_async_copy(ref.at[target], outs[d].at[pl.ds(j * span, span)], sems.at[d, j])
            copy.start()
            copies.append(copy)
    index = scal[n + hs]
    q_at = 2 * span + META * pages
    row = lax.broadcasted_iota(jnp.int32, (META, hd), 0)
    for d in range(hs):
        target = scal[n + d]
        tiles = []
        for page in range(pages):
            page_id = (index * pages + pages_ref[0, page]).astype(F32)
            value = jnp.where(row < 3, k_scale[target, page], jnp.where(row < 6, v_scale[target, page], page_id))
            hi = value.astype(BF).astype(F32)
            mid = (value - hi).astype(BF).astype(F32)
            low = value - hi - mid
            first = (row == 0) | (row == 3) | (row >= 6)
            second = (row == 1) | (row == 4)
            tiles.append(jnp.where(first, hi, jnp.where(second, mid, low)))
        for pair in range(pages // 2):
            at = 2 * span + pair * 2 * META
            both = jnp.concatenate([tiles[2 * pair], tiles[2 * pair + 1]], axis=0)
            outs[d][at : at + 2 * META, :] = both.astype(BF)
        for h in range(hp):
            at = pl.multiple_of(target * (hp * hd) + h * hd, hd)
            q = q_ref[:, :, pl.ds(at, hd)].reshape(tl, hd)
            res = res_ref[:, :, pl.ds(at, hd)].reshape(tl, hd)
            outs[d][q_at + h * tl : q_at + (h + 1) * tl, :] = q
            outs[d][q_at + rows + h * tl : q_at + rows + (h + 1) * tl, :] = res
            crosses[d][h * tl : (h + 1) * tl, :] = q
            crosses[d][rows + h * tl : rows + (h + 1) * tl, :] = res
        at = pl.multiple_of(target * hd, hd)
        f_at = q_at + 2 * rows
        outs[d][f_at : f_at + tl, :] = fk_ref[:, :, pl.ds(at, hd)].reshape(tl, hd)
        outs[d][f_at + tl : f_at + 2 * tl, :] = fv_ref[:, :, pl.ds(at, hd)].reshape(tl, hd)
    for copy in copies:
        copy.wait()


def attention_kernel(dims, scal, row_len, *refs):
    hs, _, span, pages, rows, tl, steps, group = dims
    blocks = refs[:hs]
    q_refs, refs = (blocks, refs[hs:]) if group == 0 else (refs[hs : 2 * hs], refs[2 * hs :])
    acc_ref, stat_ref, send_ref, qs, ks, vs, fk, fv, scale, lens_ref = refs
    hd = ks.shape[1]
    blk = span // pages
    nq = hs * rows
    q_at = 2 * span + META * pages
    inv_root = LOG2E / math.sqrt(hd)
    for d in range(hs):
        at = q_at if group == 0 else 0
        start = pl.multiple_of(lax.rem(scal[d], hs) * rows, rows)
        qs[pl.ds(start, rows), :] = q_refs[d][at : at + rows, :]
    f_at = q_at + 2 * rows
    fresh = fk.shape[0] // hs
    for d in range(hs):
        ks[d * span : (d + 1) * span, :] = blocks[d][0:span, :]
        vs[d * span : (d + 1) * span, :] = blocks[d][span : 2 * span, :]
        if group == 0:
            fk[d * fresh : (d + 1) * fresh, :] = blocks[d][f_at : f_at + fresh, :]
            fv[d * fresh : (d + 1) * fresh, :] = blocks[d][f_at + fresh : f_at + 2 * fresh, :]
        meta = blocks[d][2 * span : 2 * span + META * pages, :].astype(F32)
        for page in range(pages):
            m = meta[page * META : (page + 1) * META, :]
            k_row = (m[0:1] + m[1:2] + m[2:3]) * inv_root
            v_row = m[3:4] + m[4:5] + m[5:6]
            at = (d * pages + page) * META
            scale[at : at + META, :] = jnp.concatenate([k_row, v_row, m[6:7] * float(blk), m[3:8]], axis=0)
    lanes = min(256, nq)
    lane = lax.broadcasted_iota(jnp.int32, (1, nq), 1)
    rl = tl // steps
    lane_row = (lane // rows) * rl + (lane % tl) // steps
    lens = jnp.zeros((1, nq), F32)
    half = scal[group * hs] // hs
    for j in range(hs * rl):
        lens = jnp.where(lane_row == j, row_len[half * (hs * rl) + j].astype(F32), lens)
    lens_ref[...] = lens

    def chunk(c, carry):
        at = pl.multiple_of(c * lanes, lanes)
        q = qs[pl.ds(at, lanes), :]
        length = lens_ref[0:1, pl.ds(at, lanes)]
        raw = lax.dot_general(ks[...], q, NT, preferred_element_type=F32)
        inner = lax.broadcasted_iota(jnp.int32, (blk, lanes), 0).astype(F32)
        scores = []
        for page in range(hs * pages):
            k_scale = scale[page * META : page * META + 1, 0:1]
            limit = length - scale[page * META + 2 : page * META + 3, 0:1]
            part = raw[page * blk : (page + 1) * blk, :] * k_scale
            scores.append(jnp.where(inner < limit, part, NEG_FILL))
        top = jnp.full((1, lanes), TOP_FLOOR, F32)
        if group == 0:
            lane = lax.broadcasted_iota(jnp.int32, (1, lanes), 1) + at
            source = lane // rows
            token = lane % tl
            fi = lax.broadcasted_iota(jnp.int32, (fk.shape[0], 1), 0)
            f_slot = fi // fresh
            f_token = fi % fresh
            f_source = jnp.full((fk.shape[0], 1), -1, jnp.int32)
            for d in range(hs):
                f_source = jnp.where((f_slot == d) & (f_token < tl), lax.rem(scal[d], hs), f_source)
            keep = (f_source == source) & (f_token // steps == token // steps)
            keep = keep & (f_token % steps <= token % steps)
            raw_f = lax.dot_general(fk[...], q, NT, preferred_element_type=F32) * inv_root
            fresh_scores = jnp.where(keep, raw_f, NEG_FILL)
            top = jnp.maximum(top, jnp.max(fresh_scores, axis=0, keepdims=True))
        for part in scores:
            top = jnp.maximum(top, jnp.max(part, axis=0, keepdims=True))
        top = jnp.ceil(top)
        total = jnp.zeros((1, lanes), F32)
        if group == 0:
            fresh_terms = jnp.exp2(fresh_scores - top)
            total = jnp.sum(fresh_terms, axis=0, keepdims=True)
        weights = []
        for page, part in enumerate(scores):
            terms = jnp.exp2(part - top)
            total = total + jnp.sum(terms, axis=0, keepdims=True)
            weights.append((terms * scale[page * META + 1 : page * META + 2, 0:1]).astype(BF))
        weight = jnp.concatenate(weights, axis=0)
        acc = lax.dot_general(vs[...], weight, TN, preferred_element_type=F32)
        if group == 0:
            acc = acc + lax.dot_general(fv[...], fresh_terms.astype(BF), TN, preferred_element_type=F32)
        acc_ref[:, pl.ds(at, lanes)] = acc
        send_ref[0:hd, pl.ds(at, lanes)] = acc.astype(BF)
        zero = jnp.zeros((1, lanes), F32)
        stat_ref[:, pl.ds(at, lanes)] = jnp.concatenate([top, total] + [zero] * 6, axis=0)
        pieces = []
        for value in (top, total):
            hi = value.astype(BF).astype(F32)
            mid = (value - hi).astype(BF).astype(F32)
            pieces += [hi, mid, value - hi - mid]
        pieces += [zero] * 10
        send_ref[hd : hd + 16, pl.ds(at, lanes)] = jnp.concatenate(pieces, axis=0).astype(BF)
        return carry

    lax.fori_loop(0, nq // lanes, chunk, 0)


def combine_kernel(dims, scal, acc_ref, stat_ref, gain_ref, *refs):
    hs, r, rows, tl, aligned, res_at = dims
    received = refs[: r - 1]
    sources = refs[r - 1 : r - 1 + hs]
    out_ref, res = refs[r - 1 + hs :]
    hd = acc_ref.shape[0]
    hp = rows // tl
    for d in range(hs):
        start = pl.multiple_of(lax.rem(scal[d], hs) * rows, rows)
        res[pl.ds(start, rows), :] = sources[d][res_at : res_at + rows, :]
    top = stat_ref[0:1, :]
    total = stat_ref[1:2, :]
    others = []
    for ref in received:
        stats = ref[hd : hd + 16, :].astype(F32)
        o_top = stats[0:1, :] + stats[1:2, :] + stats[2:3, :]
        o_total = stats[3:4, :] + stats[4:5, :] + stats[5:6, :]
        others.append((o_top, o_total, ref))
    best = top
    for o_top, _, _ in others:
        best = jnp.maximum(best, o_top)
    factor = jnp.exp2(top - best)
    total = total * factor
    for o_top, o_total, _ in others:
        total = total + o_total * jnp.exp2(o_top - best)
    value = acc_ref[...] * (factor / total)
    for o_top, _, ref in others:
        value = value + ref[0:hd, :].astype(F32) * (jnp.exp2(o_top - best) / total)
    width = hp * hd
    gain = gain_ref[0:1, pl.ds(pl.multiple_of(lax.rem(scal[0], hs) * width, width), width)]
    for slot in range(hs):
        at = slot * rows
        part = value[:, at : at + rows].T + res[at : at + rows, :].astype(F32)
        heads = [part[h * tl : (h + 1) * tl, :] * gain[:, h * hd : (h + 1) * hd] for h in range(hp)]
        if aligned:
            for h in range(hp):
                out_ref[slot * tl : (slot + 1) * tl, h * hd : (h + 1) * hd] = heads[h].astype(BF)
        else:
            out_ref[slot] = jnp.concatenate(heads, axis=0).astype(BF)


def prefetch_kernel(count, pieces, *refs):
    ins, outs, sems = refs[:count], refs[count : 2 * count], refs[2 * count]
    copies = []
    for j in range(count):
        step = ins[j].shape[0] // pieces
        for c in range(pieces):
            at = pl.ds(c * step, step)
            copy = pltpu.make_async_copy(ins[j].at[at], outs[j].at[at], sems.at[j, c])
            copy.start()
            copies.append(copy)
    for copy in copies:
        copy.wait()


def prefetch(*arrays):
    count = len(arrays)
    pieces = 4
    return pl.pallas_call(
        functools.partial(prefetch_kernel, count, pieces),
        out_shape=[pltpu.VMEM(x.shape, x.dtype) for x in arrays],
        in_specs=[HBM] * count,
        out_specs=[VMEM] * count,
        scratch_shapes=[pltpu.SemaphoreType.DMA((count, pieces))],
        compiler_params=pltpu.CompilerParams(vmem_limit_bytes=(8 << 20) + 4096),
    )(*[hbm(x) for x in arrays])


def gate_up_kernel(dims, scal, *refs):
    first, offsets, halves, ffl, tile = dims
    if first:
        state = ()
    else:
        state, refs = refs[:2], refs[2:]
    parts = refs[: len(offsets) * halves]
    gain_ref, wg_ref, wu_ref = refs[len(parts) : len(parts) + 3]
    outs = refs[len(parts) + 3 :]
    p_all = outs[-1]
    out_ref, ssq_ref = outs[0], outs[1]
    per, width = parts[0].shape
    hs = wg_ref.shape[0] // width
    ffp = out_ref.shape[1] // 2
    starts = [pl.multiple_of(lax.rem(scal[d], hs) * width, width) for d in offsets]
    for k in range(len(offsets)):
        for j in range(halves):
            p_all[k, j * per : (j + 1) * per, :] = parts[k * halves + j][...]

    def column(at, size):
        for base, w_ref in ((0, wg_ref), (ffp, wu_ref)):
            value = None if first else state[0][:, pl.ds(base + at, size)]
            for k, start in enumerate(starts):
                term = jnp.dot(
                    p_all[k], w_ref[pl.ds(start, width), pl.ds(at, size)], preferred_element_type=F32
                )
                value = term if value is None else value + term
            out_ref[:, pl.ds(base + at, size)] = value
            if not first:
                outs[2][:, pl.ds(base + at, size)] = value.astype(BF)

    if tile == ffl:
        column(0, ffl)
    else:

        def step(i, carry):
            column(pl.multiple_of(i * tile, tile), tile)
            return carry

        lax.fori_loop(0, ffl // tile, step, 0)
    lanes = ssq_ref.shape[1]
    ssq = jnp.zeros(ssq_ref.shape, F32) if first else state[1][...]
    for k, start in enumerate(starts):
        inverse = 1.0 / gain_ref[0:1, pl.ds(start, width)]
        for c in range(width // lanes):
            cols = slice(c * lanes, (c + 1) * lanes)
            h = p_all[k, :, cols].astype(F32) * inverse[:, cols]
            ssq = ssq + h * h
    if first:
        ssq_ref[...] = ssq
    else:
        total = jnp.sum(ssq, axis=1, keepdims=True) + jnp.zeros(ssq_ref.shape, F32)
        ssq_ref[...] = total
        hi = total.astype(BF).astype(F32)
        mid = (total - hi).astype(BF).astype(F32)
        lane = lax.broadcasted_iota(jnp.int32, total.shape, 1)
        stat = jnp.where(lane == 0, hi, jnp.where(lane == 1, mid, total - hi - mid))
        outs[2][:, 2 * ffp : 2 * ffp + lanes] = stat.astype(BF)


def gate_up(offsets, scal, carry, parts, gain, w_gate, w_up, ffp):
    halves = len(parts) // len(offsets)
    per, width = parts[0].shape
    tokens = per * halves
    ffl = w_gate.shape[1]
    first = carry is None
    tile = 256 if ffl % 256 == 0 else ffl
    out_shape = [
        jax.ShapeDtypeStruct((tokens, 2 * ffp), F32),
        jax.ShapeDtypeStruct((tokens, 128), F32),
    ]
    if not first:
        out_shape.append(jax.ShapeDtypeStruct((tokens, 2 * ffp + 128), BF))
    args = [] if first else list(carry)
    args += list(parts) + [gain, resident(w_gate), resident(w_up)]
    return pl.pallas_call(
        functools.partial(gate_up_kernel, (first, offsets, halves, ffl, tile)),
        out_shape=out_shape,
        in_specs=[SMEM] + [VMEM] * len(args),
        out_specs=[VMEM] * len(out_shape),
        scratch_shapes=[pltpu.VMEM((len(offsets), tokens, width), BF)],
        compiler_params=params(8),
    )(scal, *args)


def down_kernel(dims, scal, *refs):
    first, n, hs, groups, ffl, offset, width, model = dims
    if first:
        own, ssq_ref, other, wd_ref = refs[:4]
        hidden, outs = refs[4], refs[5:]
        ffp = own.shape[1] // 2
        stat = other[:, 2 * ffp : 2 * ffp + 128].astype(F32)
        square = ssq_ref[:, 0:1] + (stat[:, 0:1] + stat[:, 1:2] + stat[:, 2:3])
        inverse = lax.rsqrt(square / model + EPSILON)
        gate = (own[:, 0:ffl] + other[:, 0:ffl].astype(F32)) * inverse
        up = (own[:, ffp : ffp + ffl] + other[:, ffp : ffp + ffl].astype(F32)) * inverse
        hidden[...] = (gate / (1.0 + jnp.exp(-gate)) * up).astype(BF)
    else:
        hidden, wd_ref, outs = refs[0], refs[1], refs[2:]
    pieces, scratch = outs[:-1], outs[-1]
    tokens = hidden.shape[0]
    block = tokens // (hs * groups)
    tile = scratch.shape[1]
    for c in range(width // tile):
        value = jnp.dot(
            hidden[...], wd_ref[:, offset + c * tile : offset + (c + 1) * tile], preferred_element_type=F32
        )
        if block % 8 == 0:
            scratch[...] = value
        for d in range(hs):
            for g in range(groups):
                first_row = g * (tokens // groups)
                if block % 8 == 0:
                    at = pl.multiple_of(first_row + scal[n + d] * block, block)
                    piece = scratch[pl.ds(at, block), :]
                else:
                    piece = value[first_row : first_row + block, :]
                    for j in range(1, hs):
                        at = first_row + j * block
                        piece = jnp.where(scal[n + d] == j, value[at : at + block, :], piece)
                pieces[d][g * block : (g + 1) * block, c * tile : (c + 1) * tile] = piece.astype(pieces[d].dtype)


def down(first, n, hs, groups, scal, args, w_down, offset, width, model):
    tokens = args[0].shape[0]
    ffl = w_down.shape[0]
    per = tokens // hs
    tile = min(width, 512)
    out_shape = [jax.ShapeDtypeStruct((tokens, ffl), BF)] if first else []
    out_shape += [jax.ShapeDtypeStruct((per, width), F32 if d == 0 else BF) for d in range(hs)]
    return pl.pallas_call(
        functools.partial(down_kernel, (first, n, hs, groups, ffl, offset, width, model)),
        out_shape=out_shape,
        in_specs=[SMEM] + [VMEM] * (len(args) + 1),
        out_specs=[VMEM] * len(out_shape),
        scratch_shapes=[pltpu.VMEM((tokens, tile), F32)],
        compiler_params=params(4),
    )(scal, *args, resident(w_down))


def own_kernel(dims, scal, gain_ref, *refs):
    n, hs, tl = dims
    parts, out_ref = refs[:-1], refs[-1]
    width = parts[0].shape[1]
    a = lax.rem(scal[n + hs], hs)
    for d in range(hs):
        part = parts[d][...].astype(F32)
        h = part[0:tl, :]
        for j in range(1, hs):
            h = jnp.where(a == j, part[j * tl : (j + 1) * tl, :], h)
        start = pl.multiple_of(lax.rem(scal[d], hs) * width, width)
        out_ref[:, pl.ds(start, width)] = h / gain_ref[0:1, pl.ds(start, width)]


def own_state(scal, gain, parts, n, hs, tl):
    half = gain.shape[1]
    return pl.pallas_call(
        functools.partial(own_kernel, (n, hs, tl)),
        out_shape=jax.ShapeDtypeStruct((tl, half), F32),
        in_specs=[SMEM] + [VMEM] * (1 + len(parts)),
        out_specs=VMEM,
        compiler_params=params(4),
    )(scal, gain, *parts)


def square_sum_kernel(r, tl, *refs):
    pieces, outs = refs[:-r], refs[-r:]
    total = pieces[0][...]
    for ref in pieces[1:]:
        total = total + ref[...].astype(F32)
    for db in range(r):
        outs[db][...] = total[db * tl : (db + 1) * tl, :].astype(outs[db].dtype)


def square_sum(pieces, r, tl):
    width = pieces[0].shape[1]
    return pl.pallas_call(
        functools.partial(square_sum_kernel, r, tl),
        out_shape=[jax.ShapeDtypeStruct((tl, width), F32 if db == 0 else BF) for db in range(r)],
        in_specs=[VMEM] * len(pieces),
        out_specs=[VMEM] * r,
        compiler_params=params(4),
    )(*pieces)


def make_body(n):
    def body(
        queries,
        fresh_keys,
        fresh_values,
        residual_in,
        cache_keys,
        cache_values,
        key_scales,
        value_scales,
        page_table,
        row_lengths,
        norm_gain,
        w_gate,
        w_up,
        w_down,
    ):
        rl, steps, half = queries.shape
        kv_heads, span, hd = cache_keys.shape
        pages = page_table.shape[1]
        hp = half // (kv_heads * hd)
        hs = math.gcd(kv_heads, n)
        assert hs == kv_heads and n * pages <= 256
        r = n // hs
        tl = rl * steps
        rows = hp * tl
        width = hp * hd
        ffl = w_gate.shape[1]
        ffp = round_up(ffl, 128)
        model = half * 2
        aligned = tl % 16 == 0
        fpad = round_up(tl, 16)
        index = lax.axis_index("seq")
        a = lax.rem(index, hs)
        b = index // hs
        pow2 = hs & (hs - 1) == 0

        def mate(x, d):
            return x ^ d if pow2 else (x + d) % hs

        def origin(x, d):
            return x ^ d if pow2 else (x - d + hs) % hs

        def shift(x, db, da):
            pairs = []
            for i in range(n):
                bi, ai = divmod(i, hs)
                pairs.append((i, ((bi + db) % r) * hs + mate(ai, da)))
            return lax.ppermute(x, "seq", pairs)

        k = jnp.arange(n + hs + 1, dtype=jnp.int32)
        k_source = ((b - k // hs + r) % r) * hs + origin(a, k % hs)
        scal = jnp.where(k < n, k_source, jnp.where(k < n + hs, mate(a, (k - n) % hs), index)).astype(jnp.int32)
        pick = lambda x, i: lax.dynamic_index_in_dim(x, i, 0, keepdims=False)

        length = 2 * span + META * pages + 2 * rows + 2 * fpad
        if aligned:
            packed = pl.pallas_call(
                functools.partial(pack_kernel, (hs, n, span, pages, rows, tl)),
                out_shape=[jax.ShapeDtypeStruct((length, hd), BF)] * hs
                + [jax.ShapeDtypeStruct((2 * rows, hd), BF)] * hs,
                in_specs=[SMEM] * 4 + [VMEM] * 4 + [HBM] * 2,
                out_specs=[VMEM] * (2 * hs),
                scratch_shapes=[pltpu.SemaphoreType.DMA((hs, 2))],
                compiler_params=params(4),
            )(
                scal,
                *[
                    hbm(x)
                    for x in (
                        key_scales,
                        value_scales,
                        page_table,
                        queries,
                        residual_in,
                        fresh_keys,
                        fresh_values,
                        cache_keys,
                        cache_values,
                    )
                ],
            )
            payloads, cross_out = packed[:hs], packed[hs:]
        else:
            page_id = (index * pages + page_table[0]).astype(F32)
            page_id = jnp.broadcast_to(page_id[None, :], (kv_heads, pages))
            zero = jnp.zeros((kv_heads, pages), F32)
            meta = jnp.stack([*split3(key_scales), *split3(value_scales), page_id, zero], axis=-1)
            meta = jnp.broadcast_to(
                meta.reshape(kv_heads, pages * META, 1), (kv_heads, pages * META, hd)
            )
            by_head = lambda x: jnp.moveaxis(x.reshape(tl, kv_heads, -1, hd), 0, 2).reshape(kv_heads, -1, hd)
            pad = ((0, 0), (0, fpad - tl), (0, 0))
            both = jnp.concatenate([by_head(queries), by_head(residual_in)], axis=1)
            payload = jnp.concatenate(
                [
                    cache_keys,
                    cache_values,
                    meta.astype(BF),
                    both,
                    jnp.pad(by_head(fresh_keys), pad),
                    jnp.pad(by_head(fresh_values), pad),
                ],
                axis=1,
            )
            targets = [mate(a, d) for d in range(hs)]
            payloads = [pick(payload, t) for t in targets]
            cross_out = [pick(both, t) for t in targets]
        blocks = [payloads[0]] + [shift(payloads[d], 0, d) for d in range(1, hs)]
        crosses = [shift(cross_out[d], db, d) for db in range(1, r) for d in range(hs)]
        wg, wu = prefetch(w_gate, w_up)
        gain2 = norm_gain.reshape(1, half)
        res_at = 2 * span + META * pages + rows
        nc = hs * rows
        per = hs * tl
        partial = []
        for g in range(r):
            attend = pl.pallas_call(
                functools.partial(attention_kernel, (hs, n, span, pages, rows, tl, steps, g)),
                out_shape=(
                    jax.ShapeDtypeStruct((hd, nc), F32),
                    jax.ShapeDtypeStruct((8, nc), F32),
                    jax.ShapeDtypeStruct((hd + 16, nc), BF),
                ),
                in_specs=[SMEM, SMEM] + [VMEM] * (hs if g == 0 else 2 * hs),
                out_specs=(VMEM, VMEM, VMEM),
                scratch_shapes=[
                    pltpu.VMEM((nc, hd), BF),
                    pltpu.VMEM((hs * span, hd), BF),
                    pltpu.VMEM((hs * span, hd), BF),
                    pltpu.VMEM((hs * fpad, hd), BF),
                    pltpu.VMEM((hs * fpad, hd), BF),
                    pltpu.VMEM((hs * pages * META, hd), F32),
                    pltpu.VMEM((1, nc), F32),
                ],
                compiler_params=params(4 if aligned else 16),
            )
            extra = [] if g == 0 else crosses[(g - 1) * hs : g * hs]
            partial.append(attend(scal, hbm(row_lengths), *blocks, *extra))
        mine = [None] * r
        arrived = {}
        for g in range(r):
            for db in range(1, r):
                arrived[(g + db) % r, db] = shift(partial[g][2], db, 0)
        for g in list(range(1, r)) + [0]:
            acc, stat, _ = partial[g]
            received = [arrived[g, db] for db in range(1, r)]
            sources = blocks if g == 0 else crosses[(g - 1) * hs : g * hs]
            p_shape = (per, width) if aligned else (hs, rows, hd)
            combine = pl.pallas_call(
                functools.partial(combine_kernel, (hs, r, rows, tl, aligned, res_at if g == 0 else rows)),
                out_shape=jax.ShapeDtypeStruct(p_shape, BF),
                in_specs=[SMEM] + [VMEM] * (3 + r - 1 + hs),
                out_specs=VMEM,
                scratch_shapes=[pltpu.VMEM((nc, hd), BF)],
                compiler_params=params(4 if aligned else 32),
            )
            p = combine(scal, acc, stat, gain2, *received, *sources)
            if not aligned:
                p = jnp.moveaxis(p.reshape(hs, hp, tl, hd), 1, 2).reshape(per, width)
            mine[g] = p
        gathered = [[shift(p, 0, d) for p in mine] for d in range(1, hs)]
        (wd,) = prefetch(w_down)
        carry = gate_up((0,), scal, None, mine, gain2, wg, wu, ffp)
        flat = [p for group in gathered for p in group]
        own, ssq, message = gate_up(tuple(range(1, hs)), scal, carry, flat, gain2, wg, wu, ffp)
        other = lax.ppermute(message, "tensor", [(0, 1), (1, 0)])

        state = own_state(scal, gain2, [mine[0]] + [g[0] for g in gathered], n, hs, tl)
        chunks = 2
        cw = half // chunks
        sums = []
        args = [own, ssq, other]
        for c in range(chunks):
            pieces = down(c == 0, n, hs, r, scal, args, wd, c * cw, cw, model)
            if c == 0:
                args, pieces = [pieces[0]], pieces[1:]
            sums.append((pieces[0], [shift(pieces[d], 0, d) for d in range(1, hs)]))
        outs = []
        for c, (total, got) in enumerate(sums):
            result, *aways = square_sum([total] + got, r, tl)
            result = state[:, c * cw : (c + 1) * cw] + result
            for db in range(1, r):
                result = result + shift(aways[db - 1], r - db, 0).astype(F32)
            outs.append(result.astype(BF))
        return jnp.concatenate(outs, axis=1).reshape(rl, steps, half)

    return body


def solution(mesh):
    in_specs = (
        P(("groups", "seq"), None, "tensor"),
        P(("groups", "seq"), None, "tensor"),
        P(("groups", "seq"), None, "tensor"),
        P(("groups", "seq"), None, "tensor"),
        P("tensor", ("groups", "seq"), None),
        P("tensor", ("groups", "seq"), None),
        P("tensor", ("groups", "seq")),
        P("tensor", ("groups", "seq")),
        P(("groups", "seq"), None),
        P("groups"),
        P("tensor"),
        P("tensor", "seq"),
        P("tensor", "seq"),
        P("seq", "tensor"),
    )
    out_specs = P(("groups", "seq"), None, "tensor")
    body = make_body(mesh.shape["seq"])
    return jax.shard_map(body, mesh=mesh, in_specs=in_specs, out_specs=out_specs, check_vma=False)
```
